128 devices in a mesh: blk: 16 (over x_lo, y, core), head: 8 (over x_hi, z).
Axes of the slice: x: 4 (x_hi: 2, x_lo: 2; x = x_hi * 2 + x_lo), y: 4, z: 4, core: 2. Of those that a mesh axis runs over, the one named last changes fastest.
Arguments:
- queries: bfloat16 [16384, 3072], P(('blk', 'head')), may hold values from -100 to 100
- keys: bfloat16 [16384, 3072], P(('blk', 'head')), may hold values from -100 to 100
- values: bfloat16 [16384, 3072], P(('blk', 'head')), may hold values from -6 to 6
- query_gain: float32 [3072], replicated, may hold values from 1 to 4
- key_gain: float32 [3072], replicated, may hold values from 0.1 to 1.9
Outputs:
- attended: bfloat16 [16384, 3072], P(('blk', 'head'))
The draws below stay inside these ranges and needn't reach their ends.
All inputs are finite; a program needn't handle non-finite values.
Results may differ from the reference program's by a relative error of at most 0.0075.
The reference program's roundings to bfloat16 on the way count: a program that leaves them out, or rounds other values in their place, can miss the bound.
Values may be sent and summed in bfloat16 or wider, within the bound.
A program may use at most 128 MiB of HBM per device.

```python
import math
import jax
import jax.numpy as jnp
from jax import lax

HEAD_DIM = 128
HEADS = 24
DIM = 3072
TOKENS = 16384


def base_noise(key, salt):
    sub = jax.random.fold_in(key, salt)
    drawn = jnp.clip(jax.random.normal(sub, (TOKENS, DIM), jnp.float32), -6.0, 6.0)
    return drawn


def draw_queries(key, part):
    scaled = base_noise(key, 11)
    return scaled.astype(jnp.bfloat16)


def draw_keys(key, part):
    scaled = base_noise(key, 12)
    return scaled.astype(jnp.bfloat16)


def level_of(stream_key, dims, pieces, low, largest):
    level = 1.0
    for position, shards_of in pieces:
        heights = jax.random.uniform(jax.random.fold_in(jax.random.fold_in(stream_key, 6), position), (shards_of,), jnp.float32, low / len(pieces), largest / len(pieces))
        level = level * jnp.repeat(jnp.exp(heights), dims[position] // shards_of).reshape((-1,) + (1,) * (len(dims) - 1 - position))
    return level


def bell_draw(stream_key, dims, scale, limit, pieces=(), kind=jnp.bfloat16):
    values = scale * jax.random.normal(stream_key, dims, jnp.float32)
    if pieces:
        values = values * level_of(stream_key, dims, pieces, -0.22, 0.18)
    return jnp.clip(values, -limit, limit).astype(kind)


def setup_inputs(seed: int = 0) -> dict:
    key_of = jax.random.split(jax.random.key(seed), 6)
    return {
        "queries": draw_queries(jax.random.fold_in(key_of[5], 71), 0),
        "keys": draw_keys(jax.random.fold_in(key_of[5], 71), 0),
        "values": bell_draw(key_of[2], (TOKENS, DIM), 1.0, 6.0, ((0, 128),)),
        "query_gain": jnp.clip(jnp.exp(jax.random.uniform(key_of[3], (DIM,), jnp.float32, math.log(1.0), math.log(4.0))), 1.0, 4.0),
        "key_gain": jnp.clip(1.0 + 0.18 * jax.random.normal(key_of[4], (DIM,), jnp.float32), 0.1, 1.9),
    }


def normalize(block, gain):
    wide = block.astype(jnp.float32)
    mean_sq = lax.optimization_barrier(jnp.mean(wide * wide, axis=-1, keepdims=True))
    return (wide * lax.rsqrt(mean_sq + 1e-06) * gain).astype(jnp.bfloat16)

def reference(queries, keys, values, query_gain, key_gain):
    normed_q = normalize(queries, query_gain).reshape(TOKENS, HEADS, HEAD_DIM)
    normed_k = normalize(keys, key_gain).reshape(TOKENS, HEADS, HEAD_DIM)
    value_heads = values.reshape(TOKENS, HEADS, HEAD_DIM)
    factor = 1.0 / math.sqrt(HEAD_DIM)
    q_size = math.gcd(TOKENS, 1024)

    def one_head(head_id):
        q_head = lax.dynamic_index_in_dim(normed_q, head_id, 1, keepdims=False)
        k_head = lax.dynamic_index_in_dim(normed_k, head_id, 1, keepdims=False)
        v_head = lax.dynamic_index_in_dim(value_heads, head_id, 1, keepdims=False)

        def one_block(block_id):
            q_rows = lax.dynamic_slice_in_dim(q_head, block_id * q_size, q_size, 0)
            scores = jnp.dot(q_rows, k_head.T, preferred_element_type=jnp.float32) * factor
            top = lax.optimization_barrier(jnp.max(scores, axis=-1, keepdims=True))
            weights = jnp.exp(scores - top)
            total = lax.optimization_barrier(jnp.sum(weights, axis=-1, keepdims=True))
            mixed = jnp.dot(weights.astype(jnp.bfloat16), v_head, preferred_element_type=jnp.float32)
            return (mixed / total).astype(jnp.bfloat16)
        blocks = lax.map(one_block, jnp.arange(TOKENS // q_size).astype(jnp.int32))
        return blocks.reshape(TOKENS, HEAD_DIM)
    result = lax.map(one_head, jnp.arange(HEADS).astype(jnp.int32))
    return jnp.transpose(result, (1, 0, 2)).reshape(TOKENS, DIM)
```

```python
import functools
import math

import jax
import jax.numpy as jnp
from jax import lax
from jax.experimental import pallas as pl
from jax.experimental.pallas import tpu as pltpu
from jax.sharding import PartitionSpec as P

HEAD_DIM = 128
EPS = 1e-06
HPG = 3
GROUPS = 8
TOK = 128
ROWS = TOK * GROUPS
BQ = 512
KEYS = 2 * ROWS
SCALE = math.log2(math.e) / math.sqrt(HEAD_DIM)
MESH = pl.DeviceIdType.MESH
PAIRS = 24
FORWARD_NEAR = {3: 0, 5: 1, 8: 2}
FORWARD_FAR = {9: 0, 11: 1, 14: 2}


def place(p):
    last = p >= 18
    chunk = p // 6
    head = jnp.where(last, (p - 18) % 3, (p % 6) // 2)
    half = jnp.where(last, 1 - (p - 18) // 3, p % 2)
    return chunk, head, half


def normed(wide, gain):
    mean_sq = jnp.mean(wide * wide, axis=-1, keepdims=True)
    return (wide * lax.rsqrt(mean_sq + EPS) * gain).astype(jnp.bfloat16)


def kernel(
    q_in, k_in, v_in, qg_ref, kg_ref, o_ref,
    qn, kn, k_all, v_all, q_all, scores, shrink, top, acc,
    part_out, part_in, lse_out, lse_in, o_out, o_in,
    kv_recv, kv_send, q_recv, q_send, in_send, part_sem, o_send, o_recv,
):
    b = lax.axis_index("blk")
    c = lax.axis_index("head")
    side = b // 8
    y = (b // 2) % 4
    core = b % 2
    other_core = (b + 1 - 2 * core, c)
    above = (side * 8 + ((y + 1) % 4) * 2 + core, c)
    below = (side * 8 + ((y + 3) % 4) * 2 + core, c)
    across = ((b + 8) % 16, c)

    def remote(src, dst, send, recv, dev):
        return pltpu.make_async_remote_copy(
            src_ref=src, dst_ref=dst, send_sem=send, recv_sem=recv,
            device_id=dev, device_id_type=MESH,
        )

    def await_bytes(ref, sem):
        pltpu.make_async_copy(ref, ref, sem).wait()

    def cols(n):
        return pl.ds(pl.multiple_of(n * HEAD_DIM, HEAD_DIM), HEAD_DIM)

    def rows_of(g):
        return pl.ds(pl.multiple_of(g * TOK, TOK), TOK)

    def k_chunk(h, slot, core_slot):
        return k_all.at[h, slot, pl.ds(core_slot * ROWS, ROWS), :]

    def v_chunk(h, slot, core_slot):
        return v_all.at[h, slot, pl.ds(core_slot * ROWS, ROWS), pl.ds(0, HEAD_DIM)]

    v_all[:, :, :, HEAD_DIM:] = jnp.ones((HPG, 4, KEYS, HEAD_DIM), jnp.bfloat16)

    barrier = pltpu.get_barrier_semaphore()
    partners = [(b, (c + d) % GROUPS) for d in range(1, GROUPS)]
    partners += [other_core, above, below, across]
    for dev in partners:
        pl.semaphore_signal(barrier, inc=1, device_id=dev, device_id_type=MESH)
    kn[...] = normed(k_in[...].astype(jnp.float32), kg_ref[...])
    pl.semaphore_wait(barrier, len(partners))

    def scatter(src, dst_of, kind, recv, h):
        mine = pltpu.make_async_copy(
            src.at[:, cols(c * HPG + h)], dst_of(rows_of(c)), recv
        )
        mine.start()
        for d in range(1, GROUPS):
            g = (c + d) % GROUPS
            remote(
                src.at[:, cols(g * HPG + h)], dst_of(rows_of(c)),
                in_send.at[kind, h], recv, (b, g),
            ).start()

    def scatter_k(h):
        scatter(kn, lambda r: k_all.at[h, 0, r, :], 0, kv_recv.at[0, h, 0, 0], h)

    def scatter_v(h):
        scatter(
            v_in, lambda r: v_all.at[h, 0, r, pl.ds(0, HEAD_DIM)], 1,
            kv_recv.at[1, h, 0, 0], h,
        )

    def scatter_q(h):
        scatter(qn, lambda r: q_all.at[h, 0, r, :], 2, q_recv.at[h, 0], h)

    scatter_k(0)
    scatter_v(0)
    qn[...] = normed(q_in[...].astype(jnp.float32), qg_ref[...])
    scatter_q(0)
    for h in range(1, HPG):
        scatter_k(h)
        scatter_v(h)
        scatter_q(h)
    acc[...] = jnp.zeros_like(acc)
    top[...] = jnp.full_like(top, -1e30)

    def send_own(h):
        await_bytes(k_chunk(h, 0, 0), kv_recv.at[0, h, 0, 0])
        await_bytes(v_chunk(h, 0, 0), kv_recv.at[1, h, 0, 0])
        for t, chunk in ((0, k_chunk), (1, v_chunk)):
            mine = chunk(h, 0, 0)
            remote(mine, chunk(h, 0, 1), kv_send.at[t, h, 0, 0],
                   kv_recv.at[t, h, 0, 1], other_core).start()
            remote(mine, chunk(h, 1, 0), kv_send.at[t, h, 0, 1],
                   kv_recv.at[t, h, 1, 0], above).start()
            remote(mine, chunk(h, 2, 0), kv_send.at[t, h, 0, 2],
                   kv_recv.at[t, h, 2, 0], below).start()
        await_bytes(q_all.at[h, 0], q_recv.at[h, 0])
        remote(q_all.at[h, 0], q_all.at[h, 1], q_send.at[h],
               q_recv.at[h, 1], across).start()

    def to_other_core(t, h, slot):
        chunk = (k_chunk, v_chunk)[t]
        remote(chunk(h, slot, 0), chunk(h, slot, 1), kv_send.at[t, h, slot, 0],
               kv_recv.at[t, h, slot, 1], other_core).start()

    def forward_near(h):
        for t, chunk in ((0, k_chunk), (1, v_chunk)):
            for slot in (1, 2):
                await_bytes(chunk(h, slot, 0), kv_recv.at[t, h, slot, 0])
        remote(k_chunk(h, 1, 0), k_chunk(h, 3, 0), kv_send.at[0, h, 1, 1],
               kv_recv.at[0, h, 3, 0], above).start()
        remote(v_chunk(h, 2, 0), v_chunk(h, 3, 0), kv_send.at[1, h, 2, 1],
               kv_recv.at[1, h, 3, 0], below).start()
        for slot in (1, 2):
            for t in (0, 1):
                to_other_core(t, h, slot)

    def forward_far(h):
        for t, chunk in ((0, k_chunk), (1, v_chunk)):
            await_bytes(chunk(h, 3, 0), kv_recv.at[t, h, 3, 0])
            to_other_core(t, h, 3)

    def score_step(p, block, slot):
        chunk, h, half = place(p)
        rows = pl.ds(block * BQ, BQ)
        s = lax.dot_general(
            q_all[h, half, rows, :], k_all[h, chunk], (((1,), (1,)), ((), ())),
            preferred_element_type=jnp.float32,
        )
        scores[slot] = s
        old = top[h, half, rows, :]
        new = jnp.maximum(old, jnp.max(s, axis=1, keepdims=True))
        top[h, half, rows, :] = new
        shrink[slot] = jnp.exp2((old - new) * SCALE)

    def value_step(p, block, slot):
        chunk, h, half = place(p)
        rows = pl.ds(block * BQ, BQ)
        weights = jnp.exp2(scores[slot] * SCALE - top[h, half, rows, :] * SCALE)
        mixed = jnp.dot(
            weights.astype(jnp.bfloat16), v_all[h, chunk],
            preferred_element_type=jnp.float32,
        )
        acc[h, half, rows, :] = acc[h, half, rows, :] * shrink[slot] + mixed

    def before(p):
        chunk, h, half = place(p)

        @pl.when(jnp.logical_and(p < 6, p % 2 == 0))
        def _():
            await_bytes(k_chunk(h, 0, 1), kv_recv.at[0, h, 0, 1])
            await_bytes(v_chunk(h, 0, 1), kv_recv.at[1, h, 0, 1])

        @pl.when(jnp.logical_and(p < 6, p % 2 == 1))
        def _():
            await_bytes(q_all.at[h, 1], q_recv.at[h, 1])

        late = jnp.logical_and(p >= 6, p < 18)

        @pl.when(jnp.logical_or(jnp.logical_and(late, p % 2 == 0),
                                jnp.logical_and(p >= 18, p < 21)))
        def _():
            await_bytes(k_chunk(h, chunk, 1), kv_recv.at[0, h, chunk, 1])
            await_bytes(v_chunk(h, chunk, 1), kv_recv.at[1, h, chunk, 1])

    def finish_block(h, half, block):
        rows = pl.ds(block * BQ, BQ)
        total = acc[h, half, rows, HEAD_DIM:]
        mean = acc[h, half, rows, :HEAD_DIM] / total
        lse = top[h, half, rows, :] * SCALE + jnp.log2(total)
        return mean, lse

    def send_part(h):
        for block in range(ROWS // BQ):
            rows = pl.ds(block * BQ, BQ)
            mean, lse = finish_block(h, 1, block)
            part_out[h, rows, :] = mean.astype(jnp.bfloat16)
            lse_out[h, :, rows] = jnp.transpose(lse)[:8]
        remote(part_out.at[h], part_in.at[h], part_sem.at[0, h, 0],
               part_sem.at[1, h, 0], across).start()
        remote(lse_out.at[h], lse_in.at[h], part_sem.at[0, h, 1],
               part_sem.at[1, h, 1], across).start()

    def send_result(h):
        await_bytes(part_in.at[h], part_sem.at[1, h, 0])
        await_bytes(lse_in.at[h], part_sem.at[1, h, 1])
        for block in range(ROWS // BQ):
            rows = pl.ds(block * BQ, BQ)
            mean, lse = finish_block(h, 0, block)
            row = jnp.broadcast_to(lse_in[h, 0:1, rows], (HEAD_DIM, BQ))
            lse2 = jnp.transpose(row)
            peak = jnp.maximum(lse, lse2)
            w1 = jnp.exp2(lse - peak)
            w2 = jnp.exp2(lse2 - peak)
            both = mean * w1 + part_in[h, rows, :].astype(jnp.float32) * w2
            o_out[h, rows, :] = (both / (w1 + w2)).astype(jnp.bfloat16)
        target = cols(c * HPG + h)
        pltpu.make_async_copy(
            o_out.at[h, rows_of(c), :], o_in.at[:, target], o_recv.at[h]
        ).start()
        for d in range(1, GROUPS):
            g = (c + d) % GROUPS
            remote(o_out.at[h, rows_of(g), :], o_in.at[:, target],
                   o_send.at[h], o_recv.at[h], (b, g)).start()

    send_own(0)
    before(0)
    score_step(0, 0, 0)

    def pair(p, carry):
        score_step(p, 1, 1)
        value_step(p, 0, 0)

        for h in range(1, HPG):
            @pl.when(p == 2 * h - 1)
            def _():
                send_own(h)
        for at, h in FORWARD_NEAR.items():
            @pl.when(p == at)
            def _():
                forward_near(h)
        for at, h in FORWARD_FAR.items():
            @pl.when(p == at)
            def _():
                forward_far(h)

        nxt = jnp.minimum(p + 1, PAIRS - 1)

        @pl.when(p < PAIRS - 1)
        def _():
            before(nxt)

        score_step_next(p)
        value_step(p, 1, 1)

        for h in range(HPG):
            @pl.when(p == 18 + h)
            def _():
                send_part(h)

            @pl.when(p == 21 + h)
            def _():
                send_result(h)
        return carry

    def score_step_next(p):
        score_step(p + 1, 0, 0)

    lax.fori_loop(0, PAIRS - 1, pair, 0)
    p = PAIRS - 1
    score_step(p, 1, 1)
    value_step(p, 0, 0)
    value_step(p, 1, 1)
    send_result(HPG - 1)

    for h in range(HPG):
        await_bytes(o_out.at[h], o_recv.at[h])
    o_ref[...] = o_in[...]

    seven = pl.ds(0, (GROUPS - 1) * TOK)
    for h in range(HPG):
        await_bytes(o_out.at[h, seven, :], o_send.at[h])
        await_bytes(part_out.at[h], part_sem.at[0, h, 0])
        await_bytes(lse_out.at[h], part_sem.at[0, h, 1])
        await_bytes(q_all.at[h, 0], q_send.at[h])
        for kind in range(3):
            await_bytes(o_out.at[h, seven, :], in_send.at[kind, h])
        for t, chunk in ((0, k_chunk), (1, v_chunk)):
            for i in range(3):
                await_bytes(chunk(h, 0, 0), kv_send.at[t, h, 0, i])
            for slot in (1, 2, 3):
                await_bytes(chunk(h, slot, 0), kv_send.at[t, h, slot, 0])
        await_bytes(k_chunk(h, 1, 0), kv_send.at[0, h, 1, 1])
        await_bytes(v_chunk(h, 2, 0), kv_send.at[1, h, 2, 1])


def shards(queries, keys, values, query_gain, key_gain):
    bf16, f32 = jnp.bfloat16, jnp.float32
    dma = pltpu.SemaphoreType.DMA
    width = queries.shape[1]
    halves = (HPG, 2, ROWS)
    return pl.pallas_call(
        kernel,
        out_shape=jax.ShapeDtypeStruct((TOK, width), bf16),
        in_specs=[pl.BlockSpec(memory_space=pltpu.VMEM)] * 5,
        out_specs=pl.BlockSpec(memory_space=pltpu.VMEM),
        scratch_shapes=[
            pltpu.VMEM((TOK, width), bf16),
            pltpu.VMEM((TOK, width), bf16),
            pltpu.VMEM((HPG, 4, KEYS, HEAD_DIM), bf16),
            pltpu.VMEM((HPG, 4, KEYS, 2 * HEAD_DIM), bf16),
            pltpu.VMEM((*halves, HEAD_DIM), bf16),
            pltpu.VMEM((2, BQ, KEYS), f32),
            pltpu.VMEM((2, BQ, 1), f32),
            pltpu.VMEM((*halves, 1), f32),
            pltpu.VMEM((*halves, 2 * HEAD_DIM), f32),
            pltpu.VMEM((HPG, ROWS, HEAD_DIM), bf16),
            pltpu.VMEM((HPG, ROWS, HEAD_DIM), bf16),
            pltpu.VMEM((HPG, 8, ROWS), f32),
            pltpu.VMEM((HPG, 8, ROWS), f32),
            pltpu.VMEM((HPG, ROWS, HEAD_DIM), bf16),
            pltpu.VMEM((TOK, width), bf16),
            dma((2, HPG, 4, 2)),
            dma((2, HPG, 4, 3)),
            dma((HPG, 2)),
            dma((HPG,)),
            dma((3, HPG)),
            dma((2, HPG, 2)),
            dma((HPG,)),
            dma((HPG,)),
        ],
        compiler_params=pltpu.CompilerParams(
            collective_id=0, has_side_effects=True, vmem_limit_bytes=60 << 20
        ),
    )(queries, keys, values, query_gain.reshape(1, width), key_gain.reshape(1, width))


def solution(mesh):
    rows = P(("blk", "head"), None)
    return jax.shard_map(
        shards, mesh=mesh, in_specs=(rows, rows, rows, P(), P()), out_specs=rows,
        check_vma=False,
    )
```

```python
import functools
import math

import jax
import jax.numpy as jnp
from jax import lax
from jax.experimental import pallas as pl
from jax.experimental.pallas import tpu as pltpu
from jax.sharding import PartitionSpec as P

HEAD_DIM = 128
EPS = 1e-06
HPG = 3
GROUPS = 8
TOK = 128
ROWS = TOK * GROUPS
BQ = 512
KEYS = 2 * ROWS
SCALE = math.log2(math.e) / math.sqrt(HEAD_DIM)
MESH = pl.DeviceIdType.MESH
PAIRS = 24
FORWARD_NEAR = {3: 0, 5: 1, 8: 2}
FORWARD_FAR = {9: 0, 11: 1, 14: 2}


def place(p):
    last = p >= 18
    chunk = p // 6
    head = jnp.where(last, (p - 18) % 3, (p % 6) // 2)
    half = jnp.where(last, 1 - (p - 18) // 3, p % 2)
    return chunk, head, half


def normed(wide, gain):
    mean_sq = jnp.mean(wide * wide, axis=-1, keepdims=True)
    return (wide * lax.rsqrt(mean_sq + EPS) * gain).astype(jnp.bfloat16)


def kernel(
    q_in, k_in, v_in, qg_ref, kg_ref, o_ref,
    qn, kn, k_all, v_all, q_all, scores, shrink, peak, top, acc,
    part_out, part_in, lse_out, lse_in, o_out, o_in,
    kv_recv, kv_send, q_recv, q_send, in_send, part_sem, o_send, o_recv,
):
    b = lax.axis_index("blk")
    c = lax.axis_index("head")
    side = b // 8
    y = (b // 2) % 4
    core = b % 2
    other_core = (b + 1 - 2 * core, c)
    above = (side * 8 + ((y + 1) % 4) * 2 + core, c)
    below = (side * 8 + ((y + 3) % 4) * 2 + core, c)
    across = ((b + 8) % 16, c)

    def remote(src, dst, send, recv, dev):
        return pltpu.make_async_remote_copy(
            src_ref=src, dst_ref=dst, send_sem=send, recv_sem=recv,
            device_id=dev, device_id_type=MESH,
        )

    def await_bytes(ref, sem):
        pltpu.make_async_copy(ref, ref, sem).wait()

    def cols(n):
        return pl.ds(pl.multiple_of(n * HEAD_DIM, HEAD_DIM), HEAD_DIM)

    def rows_of(g):
        return pl.ds(pl.multiple_of(g * TOK, TOK), TOK)

    def k_chunk(h, slot, core_slot):
        return k_all.at[h, slot, pl.ds(core_slot * ROWS, ROWS), :]

    def v_chunk(h, slot, core_slot):
        return v_all.at[h, slot, pl.ds(core_slot * ROWS, ROWS), pl.ds(0, HEAD_DIM)]

    v_all[:, :, :, HEAD_DIM:] = jnp.ones((HPG, 4, KEYS, HEAD_DIM), jnp.bfloat16)

    barrier = pltpu.get_barrier_semaphore()
    partners = [(b, (c + d) % GROUPS) for d in range(1, GROUPS)]
    partners += [other_core, above, below, across]
    for dev in partners:
        pl.semaphore_signal(barrier, inc=1, device_id=dev, device_id_type=MESH)
    kn[...] = normed(k_in[...].astype(jnp.float32), kg_ref[...])
    pl.semaphore_wait(barrier, len(partners))

    def scatter(src, dst_of, kind, recv, h):
        mine = pltpu.make_async_copy(
            src.at[:, cols(c * HPG + h)], dst_of(rows_of(c)), recv
        )
        mine.start()
        for d in range(1, GROUPS):
            g = (c + d) % GROUPS
            remote(
                src.at[:, cols(g * HPG + h)], dst_of(rows_of(c)),
                in_send.at[kind, h], recv, (b, g),
            ).start()

    def scatter_k(h):
        scatter(kn, lambda r: k_all.at[h, 0, r, :], 0, kv_recv.at[0, h, 0, 0], h)

    def scatter_v(h):
        scatter(
            v_in, lambda r: v_all.at[h, 0, r, pl.ds(0, HEAD_DIM)], 1,
            kv_recv.at[1, h, 0, 0], h,
        )

    def scatter_q(h):
        scatter(qn, lambda r: q_all.at[h, 0, r, :], 2, q_recv.at[h, 0], h)

    scatter_k(0)
    scatter_v(0)
    qn[...] = normed(q_in[...].astype(jnp.float32), qg_ref[...])
    scatter_q(0)
    acc[...] = jnp.zeros_like(acc)
    top[...] = jnp.full_like(top, -1e30)

    def send_own(h):
        await_bytes(k_chunk(h, 0, 0), kv_recv.at[0, h, 0, 0])
        await_bytes(v_chunk(h, 0, 0), kv_recv.at[1, h, 0, 0])
        for t, chunk in ((0, k_chunk), (1, v_chunk)):
            mine = chunk(h, 0, 0)
            remote(mine, chunk(h, 0, 1), kv_send.at[t, h, 0, 0],
                   kv_recv.at[t, h, 0, 1], other_core).start()
            remote(mine, chunk(h, 1, 0), kv_send.at[t, h, 0, 1],
                   kv_recv.at[t, h, 1, 0], above).start()
            remote(mine, chunk(h, 2, 0), kv_send.at[t, h, 0, 2],
                   kv_recv.at[t, h, 2, 0], below).start()
        await_bytes(q_all.at[h, 0], q_recv.at[h, 0])
        remote(q_all.at[h, 0], q_all.at[h, 1], q_send.at[h],
               q_recv.at[h, 1], across).start()

    def to_other_core(t, h, slot):
        chunk = (k_chunk, v_chunk)[t]
        remote(chunk(h, slot, 0), chunk(h, slot, 1), kv_send.at[t, h, slot, 0],
               kv_recv.at[t, h, slot, 1], other_core).start()

    def forward_near(h):
        for t, chunk in ((0, k_chunk), (1, v_chunk)):
            for slot in (1, 2):
                await_bytes(chunk(h, slot, 0), kv_recv.at[t, h, slot, 0])
        remote(k_chunk(h, 1, 0), k_chunk(h, 3, 0), kv_send.at[0, h, 1, 1],
               kv_recv.at[0, h, 3, 0], above).start()
        remote(v_chunk(h, 2, 0), v_chunk(h, 3, 0), kv_send.at[1, h, 2, 1],
               kv_recv.at[1, h, 3, 0], below).start()
        for slot in (1, 2):
            for t in (0, 1):
                to_other_core(t, h, slot)

    def forward_far(h):
        for t, chunk in ((0, k_chunk), (1, v_chunk)):
            await_bytes(chunk(h, 3, 0), kv_recv.at[t, h, 3, 0])
            to_other_core(t, h, 3)

    def score_step(p, block, slot):
        chunk, h, half = place(p)
        rows = pl.ds(block * BQ, BQ)
        s = lax.dot_general(
            q_all[h, half, rows, :], k_all[h, chunk], (((1,), (1,)), ((), ())),
            preferred_element_type=jnp.float32,
        )
        scores[slot] = s
        old = top[h, half, rows, :]
        new = jnp.maximum(old, jnp.max(s, axis=1, keepdims=True))
        top[h, half, rows, :] = new
        peak[slot] = new * SCALE
        shrink[slot] = jnp.exp2((old - new) * SCALE)

    def value_step(p, block, slot):
        chunk, h, half = place(p)
        rows = pl.ds(block * BQ, BQ)
        weights = jnp.exp2(scores[slot] * SCALE - peak[slot])
        mixed = jnp.dot(
            weights.astype(jnp.bfloat16), v_all[h, chunk],
            preferred_element_type=jnp.float32,
        )
        acc[h, half, rows, :] = acc[h, half, rows, :] * shrink[slot] + mixed

    def before(p):
        chunk, h, half = place(p)

        @pl.when(jnp.logical_and(p < 6, p % 2 == 0))
        def _():
            await_bytes(k_chunk(h, 0, 1), kv_recv.at[0, h, 0, 1])
            await_bytes(v_chunk(h, 0, 1), kv_recv.at[1, h, 0, 1])

        @pl.when(jnp.logical_and(p < 6, p % 2 == 1))
        def _():
            await_bytes(q_all.at[h, 1], q_recv.at[h, 1])

        late = jnp.logical_and(p >= 6, p < 18)

        @pl.when(jnp.logical_or(jnp.logical_and(late, p % 2 == 0),
                                jnp.logical_and(p >= 18, p < 21)))
        def _():
            await_bytes(k_chunk(h, chunk, 1), kv_recv.at[0, h, chunk, 1])
            await_bytes(v_chunk(h, chunk, 1), kv_recv.at[1, h, chunk, 1])

    def finish_block(h, half, block):
        rows = pl.ds(block * BQ, BQ)
        total = acc[h, half, rows, HEAD_DIM:]
        mean = acc[h, half, rows, :HEAD_DIM] / total
        lse = top[h, half, rows, :] * SCALE + jnp.log2(total)
        return mean, lse

    def send_part(h):
        for block in range(ROWS // BQ):
            rows = pl.ds(block * BQ, BQ)
            mean, lse = finish_block(h, 1, block)
            part_out[h, rows, :] = mean.astype(jnp.bfloat16)
            lse_out[h, :, rows] = jnp.transpose(lse)[:8]
        remote(part_out.at[h], part_in.at[h], part_sem.at[0, h, 0],
               part_sem.at[1, h, 0], across).start()
        remote(lse_out.at[h], lse_in.at[h], part_sem.at[0, h, 1],
               part_sem.at[1, h, 1], across).start()

    def send_result(h):
        await_bytes(part_in.at[h], part_sem.at[1, h, 0])
        await_bytes(lse_in.at[h], part_sem.at[1, h, 1])
        for block in range(ROWS // BQ):
            rows = pl.ds(block * BQ, BQ)
            mean, lse = finish_block(h, 0, block)
            row = jnp.broadcast_to(lse_in[h, 0:1, rows], (HEAD_DIM, BQ))
            lse2 = jnp.transpose(row)
            high = jnp.maximum(lse, lse2)
            w1 = jnp.exp2(lse - high)
            w2 = jnp.exp2(lse2 - high)
            both = mean * w1 + part_in[h, rows, :].astype(jnp.float32) * w2
            o_out[h, rows, :] = (both / (w1 + w2)).astype(jnp.bfloat16)
        target = cols(c * HPG + h)
        pltpu.make_async_copy(
            o_out.at[h, rows_of(c), :], o_in.at[:, target], o_recv.at[h]
        ).start()
        for d in range(1, GROUPS):
            g = (c + d) % GROUPS
            remote(o_out.at[h, rows_of(g), :], o_in.at[:, target],
                   o_send.at[h], o_recv.at[h], (b, g)).start()

    seven = pl.ds(0, (GROUPS - 1) * TOK)

    def scatter_done(h):
        for kind in range(3):
            await_bytes(o_out.at[h, seven, :], in_send.at[kind, h])

    scatter_done(0)
    scatter_k(1)
    scatter_v(1)
    scatter_q(1)
    send_own(0)
    scatter_done(1)
    scatter_k(2)
    scatter_v(2)
    scatter_q(2)
    before(0)
    score_step(0, 0, 0)

    def pair(p, carry):
        score_step(p, 1, 1)
        value_step(p, 0, 0)

        for h in range(1, HPG):
            @pl.when(p == 2 * h - 1)
            def _():
                send_own(h)
        for at, h in FORWARD_NEAR.items():
            @pl.when(p == at)
            def _():
                forward_near(h)
        for at, h in FORWARD_FAR.items():
            @pl.when(p == at)
            def _():
                forward_far(h)

        nxt = jnp.minimum(p + 1, PAIRS - 1)

        @pl.when(p < PAIRS - 1)
        def _():
            before(nxt)

        score_step_next(p)
        value_step(p, 1, 1)

        for h in range(HPG):
            @pl.when(p == 18 + h)
            def _():
                send_part(h)

            @pl.when(p == 21 + h)
            def _():
                send_result(h)
        return carry

    def score_step_next(p):
        score_step(p + 1, 0, 0)

    lax.fori_loop(0, PAIRS - 1, pair, 0)
    p = PAIRS - 1
    score_step(p, 1, 1)
    value_step(p, 0, 0)
    value_step(p, 1, 1)
    send_result(HPG - 1)

    for h in range(HPG):
        await_bytes(o_out.at[h], o_recv.at[h])
    o_ref[...] = o_in[...]

    scatter_done(2)
    for h in range(HPG):
        await_bytes(o_out.at[h, seven, :], o_send.at[h])
        await_bytes(part_out.at[h], part_sem.at[0, h, 0])
        await_bytes(lse_out.at[h], part_sem.at[0, h, 1])
        await_bytes(q_all.at[h, 0], q_send.at[h])
        for t, chunk in ((0, k_chunk), (1, v_chunk)):
            for i in range(3):
                await_bytes(chunk(h, 0, 0), kv_send.at[t, h, 0, i])
            for slot in (1, 2, 3):
                await_bytes(chunk(h, slot, 0), kv_send.at[t, h, slot, 0])
        await_bytes(k_chunk(h, 1, 0), kv_send.at[0, h, 1, 1])
        await_bytes(v_chunk(h, 2, 0), kv_send.at[1, h, 2, 1])


def shards(queries, keys, values, query_gain, key_gain):
    bf16, f32 = jnp.bfloat16, jnp.float32
    dma = pltpu.SemaphoreType.DMA
    width = queries.shape[1]
    halves = (HPG, 2, ROWS)
    return pl.pallas_call(
        kernel,
        out_shape=jax.ShapeDtypeStruct((TOK, width), bf16),
        in_specs=[pl.BlockSpec(memory_space=pltpu.VMEM)] * 5,
        out_specs=pl.BlockSpec(memory_space=pltpu.VMEM),
        scratch_shapes=[
            pltpu.VMEM((TOK, width), bf16),
            pltpu.VMEM((TOK, width), bf16),
            pltpu.VMEM((HPG, 4, KEYS, HEAD_DIM), bf16),
            pltpu.VMEM((HPG, 4, KEYS, 2 * HEAD_DIM), bf16),
            pltpu.VMEM((*halves, HEAD_DIM), bf16),
            pltpu.VMEM((2, BQ, KEYS), f32),
            pltpu.VMEM((2, BQ, 1), f32),
            pltpu.VMEM((2, BQ, 1), f32),
            pltpu.VMEM((*halves, 1), f32),
            pltpu.VMEM((*halves, 2 * HEAD_DIM), f32),
            pltpu.VMEM((HPG, ROWS, HEAD_DIM), bf16),
            pltpu.VMEM((HPG, ROWS, HEAD_DIM), bf16),
            pltpu.VMEM((HPG, 8, ROWS), f32),
            pltpu.VMEM((HPG, 8, ROWS), f32),
            pltpu.VMEM((HPG, ROWS, HEAD_DIM), bf16),
            pltpu.VMEM((TOK, width), bf16),
            dma((2, HPG, 4, 2)),
            dma((2, HPG, 4, 3)),
            dma((HPG, 2)),
            dma((HPG,)),
            dma((3, HPG)),
            dma((2, HPG, 2)),
            dma((HPG,)),
            dma((HPG,)),
        ],
        compiler_params=pltpu.CompilerParams(
            collective_id=0, has_side_effects=True, vmem_limit_bytes=60 << 20
        ),
    )(queries, keys, values, query_gain.reshape(1, width), key_gain.reshape(1, width))


def solution(mesh):
    rows = P(("blk", "head"), None)
    return jax.shard_map(
        shards, mesh=mesh, in_specs=(rows, rows, rows, P(), P()), out_specs=rows,
        check_vma=False,
    )
```

```python
import functools
import math

import jax
import jax.numpy as jnp
from jax import lax
from jax.experimental import pallas as pl
from jax.experimental.pallas import tpu as pltpu
from jax.sharding import PartitionSpec as P

HEAD_DIM = 128
EPS = 1e-06
HPG = 3
GROUPS = 8
TOK = 128
ROWS = TOK * GROUPS
BQ = 512
KEYS = 2 * ROWS
SCALE = math.log2(math.e) / math.sqrt(HEAD_DIM)
MESH = pl.DeviceIdType.MESH
ORDER = (
    (0, 0, 0), (0, 0, 1), (1, 0, 0), (0, 1, 0), (0, 1, 1), (0, 2, 0),
    (0, 2, 1), (1, 0, 1), (2, 0, 0), (1, 1, 0), (1, 1, 1), (1, 2, 0),
    (1, 2, 1), (0, 3, 1), (2, 0, 1), (1, 3, 1), (2, 1, 0), (2, 1, 1),
    (2, 2, 0), (2, 2, 1), (2, 3, 1), (0, 3, 0), (1, 3, 0), (2, 3, 0),
)
PAIRS = len(ORDER)
FORWARD_NEAR = {7: 1, 11: 2}
FORWARD_FAR = {8: 0, 12: 1, 17: 2}


def first_uses(key):
    seen, firsts = set(), []
    for p, entry in enumerate(ORDER):
        if key(entry) is not None and key(entry) not in seen:
            seen.add(key(entry))
            firsts.append(p)
    return firsts


CHUNK_FIRST = first_uses(lambda e: e[:2])
ACROSS_FIRST = first_uses(lambda e: e[0] if e[2] else None)


def one_of(u, options):
    return functools.reduce(jnp.logical_or, [u == o for o in options])


def place(p):
    def column(i):
        value = 0
        for v in sorted({e[i] for e in ORDER} - {0}):
            value = jnp.where(one_of(p, [n for n, e in enumerate(ORDER) if e[i] == v]), v, value)
        return value

    return column(1), column(0), column(2)


def normed(wide, gain):
    mean_sq = jnp.mean(wide * wide, axis=-1, keepdims=True)
    return (wide * lax.rsqrt(mean_sq + EPS) * gain).astype(jnp.bfloat16)


def kernel(
    q_in, k_in, v_in, qg_ref, kg_ref, o_ref,
    qn, kn, k_all, v_all, q_all, scores, shrink, peak, top, acc,
    part_out, part_in, lse_out, lse_in, o_out, o_in,
    kv_recv, kv_send, q_recv, q_send, in_send, part_sem, o_send, o_recv,
):
    b = lax.axis_index("blk")
    c = lax.axis_index("head")
    side = b // 8
    y = (b // 2) % 4
    core = b % 2
    other_core = (b + 1 - 2 * core, c)
    above = (side * 8 + ((y + 1) % 4) * 2 + core, c)
    below = (side * 8 + ((y + 3) % 4) * 2 + core, c)
    across = ((b + 8) % 16, c)

    def remote(src, dst, send, recv, dev):
        return pltpu.make_async_remote_copy(
            src_ref=src, dst_ref=dst, send_sem=send, recv_sem=recv,
            device_id=dev, device_id_type=MESH,
        )

    def await_bytes(ref, sem):
        pltpu.make_async_copy(ref, ref, sem).wait()

    def cols(n):
        return pl.ds(pl.multiple_of(n * HEAD_DIM, HEAD_DIM), HEAD_DIM)

    def rows_of(g):
        return pl.ds(pl.multiple_of(g * TOK, TOK), TOK)

    def k_chunk(h, slot, core_slot):
        return k_all.at[h, slot, pl.ds(core_slot * ROWS, ROWS), :]

    def v_chunk(h, slot, core_slot):
        return v_all.at[h, slot, pl.ds(core_slot * ROWS, ROWS), pl.ds(0, HEAD_DIM)]

    v_all[:, :, :, HEAD_DIM:] = jnp.ones((HPG, 4, KEYS, HEAD_DIM), jnp.bfloat16)

    barrier = pltpu.get_barrier_semaphore()
    partners = [(b, (c + d) % GROUPS) for d in range(1, GROUPS)]
    partners += [other_core, above, below, across]
    for dev in partners:
        pl.semaphore_signal(barrier, inc=1, device_id=dev, device_id_type=MESH)
    kn[...] = normed(k_in[...].astype(jnp.float32), kg_ref[...])
    qn[...] = normed(q_in[...].astype(jnp.float32), qg_ref[...])
    pl.semaphore_wait(barrier, len(partners))

    def scatter(src, dst_of, kind, recv, h):
        mine = pltpu.make_async_copy(
            src.at[:, cols(c * HPG + h)], dst_of(rows_of(c)), recv
        )
        mine.start()
        for d in range(1, GROUPS):
            g = (c + d) % GROUPS
            remote(
                src.at[:, cols(g * HPG + h)], dst_of(rows_of(c)),
                in_send.at[kind, h], recv, (b, g),
            ).start()

    def scatter_k(h):
        scatter(kn, lambda r: k_all.at[h, 0, r, :], 0, kv_recv.at[0, h, 0, 0], h)

    def scatter_v(h):
        scatter(
            v_in, lambda r: v_all.at[h, 0, r, pl.ds(0, HEAD_DIM)], 1,
            kv_recv.at[1, h, 0, 0], h,
        )

    def scatter_q(h):
        scatter(qn, lambda r: q_all.at[h, 0, r, :], 2, q_recv.at[h, 0], h)

    scatter_q(0)
    scatter_k(0)
    scatter_v(0)
    acc[...] = jnp.zeros_like(acc)
    top[...] = jnp.full_like(top, -1e30)

    def send_own(h):
        await_bytes(k_chunk(h, 0, 0), kv_recv.at[0, h, 0, 0])
        await_bytes(v_chunk(h, 0, 0), kv_recv.at[1, h, 0, 0])
        for t, chunk in ((0, k_chunk), (1, v_chunk)):
            mine = chunk(h, 0, 0)
            remote(mine, chunk(h, 0, 1), kv_send.at[t, h, 0, 0],
                   kv_recv.at[t, h, 0, 1], other_core).start()
            remote(mine, chunk(h, 1, 0), kv_send.at[t, h, 0, 1],
                   kv_recv.at[t, h, 1, 0], above).start()
            remote(mine, chunk(h, 2, 0), kv_send.at[t, h, 0, 2],
                   kv_recv.at[t, h, 2, 0], below).start()

    def send_across(h):
        await_bytes(q_all.at[h, 0], q_recv.at[h, 0])
        remote(q_all.at[h, 0], q_all.at[h, 1], q_send.at[h],
               q_recv.at[h, 1], across).start()

    def to_other_core(t, h, slot):
        chunk = (k_chunk, v_chunk)[t]
        remote(chunk(h, slot, 0), chunk(h, slot, 1), kv_send.at[t, h, slot, 0],
               kv_recv.at[t, h, slot, 1], other_core).start()

    def forward_near(h):
        for t, chunk in ((0, k_chunk), (1, v_chunk)):
            for slot in (1, 2):
                await_bytes(chunk(h, slot, 0), kv_recv.at[t, h, slot, 0])
        remote(k_chunk(h, 1, 0), k_chunk(h, 3, 0), kv_send.at[0, h, 1, 1],
               kv_recv.at[0, h, 3, 0], above).start()
        remote(v_chunk(h, 2, 0), v_chunk(h, 3, 0), kv_send.at[1, h, 2, 1],
               kv_recv.at[1, h, 3, 0], below).start()
        for slot in (1, 2):
            for t in (0, 1):
                to_other_core(t, h, slot)

    def forward_far(h):
        for t, chunk in ((0, k_chunk), (1, v_chunk)):
            await_bytes(chunk(h, 3, 0), kv_recv.at[t, h, 3, 0])
            to_other_core(t, h, 3)

    def score_step(p, block, slot):
        chunk, h, half = place(p)
        rows = pl.ds(block * BQ, BQ)
        s = lax.dot_general(
            q_all[h, half, rows, :], k_all[h, chunk], (((1,), (1,)), ((), ())),
            preferred_element_type=jnp.float32,
        )
        scores[slot] = s
        old = top[h, half, rows, :]
        new = jnp.maximum(old, jnp.max(s, axis=1, keepdims=True))
        top[h, half, rows, :] = new
        peak[slot] = new * SCALE
        shrink[slot] = jnp.exp2((old - new) * SCALE)

    def value_step(p, block, slot):
        chunk, h, half = place(p)
        rows = pl.ds(block * BQ, BQ)
        weights = jnp.exp2(scores[slot] * SCALE - peak[slot])
        mixed = jnp.dot(
            weights.astype(jnp.bfloat16), v_all[h, chunk],
            preferred_element_type=jnp.float32,
        )
        acc[h, half, rows, :] = acc[h, half, rows, :] * shrink[slot] + mixed

    def before(p):
        chunk, h, half = place(p)

        @pl.when(one_of(p, CHUNK_FIRST))
        def _():
            await_bytes(k_chunk(h, chunk, 1), kv_recv.at[0, h, chunk, 1])
            await_bytes(v_chunk(h, chunk, 1), kv_recv.at[1, h, chunk, 1])

        @pl.when(one_of(p, ACROSS_FIRST))
        def _():
            await_bytes(q_all.at[h, 1], q_recv.at[h, 1])

    def finish_block(h, half, block):
        rows = pl.ds(block * BQ, BQ)
        total = acc[h, half, rows, HEAD_DIM:]
        mean = acc[h, half, rows, :HEAD_DIM] / total
        lse = top[h, half, rows, :] * SCALE + jnp.log2(total)
        return mean, lse

    def send_part(h):
        for block in range(ROWS // BQ):
            rows = pl.ds(block * BQ, BQ)
            mean, lse = finish_block(h, 1, block)
            part_out[h, rows, :] = mean.astype(jnp.bfloat16)
            lse_out[h, :, rows] = jnp.transpose(lse)[:8]
        remote(part_out.at[h], part_in.at[h], part_sem.at[0, h, 0],
               part_sem.at[1, h, 0], across).start()
        remote(lse_out.at[h], lse_in.at[h], part_sem.at[0, h, 1],
               part_sem.at[1, h, 1], across).start()

    def send_result(h):
        await_bytes(part_in.at[h], part_sem.at[1, h, 0])
        await_bytes(lse_in.at[h], part_sem.at[1, h, 1])
        for block in range(ROWS // BQ):
            rows = pl.ds(block * BQ, BQ)
            mean, lse = finish_block(h, 0, block)
            row = jnp.broadcast_to(lse_in[h, 0:1, rows], (HEAD_DIM, BQ))
            lse2 = jnp.transpose(row)
            high = jnp.maximum(lse, lse2)
            w1 = jnp.exp2(lse - high)
            w2 = jnp.exp2(lse2 - high)
            both = mean * w1 + part_in[h, rows, :].astype(jnp.float32) * w2
            o_out[h, rows, :] = (both / (w1 + w2)).astype(jnp.bfloat16)
        target = cols(c * HPG + h)
        pltpu.make_async_copy(
            o_out.at[h, rows_of(c), :], o_in.at[:, target], o_recv.at[h]
        ).start()
        for d in range(1, GROUPS):
            g = (c + d) % GROUPS
            remote(o_out.at[h, rows_of(g), :], o_in.at[:, target],
                   o_send.at[h], o_recv.at[h], (b, g)).start()

    seven = pl.ds(0, (GROUPS - 1) * TOK)

    def sent(kind, h):
        await_bytes(o_out.at[h, seven, :], in_send.at[kind, h])

    send_across(0)
    for kind in range(3):
        sent(kind, 0)
    scatter_k(1)
    scatter_v(1)
    scatter_q(1)
    send_own(0)
    before(0)
    score_step(0, 0, 0)

    def pair(p, carry):
        score_step(p, 1, 1)
        value_step(p, 0, 0)

        @pl.when(p == 0)
        def _():
            sent(0, 1)
            scatter_k(2)

        @pl.when(p == 1)
        def _():
            sent(1, 1)
            scatter_v(2)
            sent(2, 1)
            scatter_q(2)
            send_own(1)
            send_across(1)
            forward_near(0)

        @pl.when(p == 4)
        def _():
            send_own(2)
            send_across(2)

        for at, h in FORWARD_NEAR.items():
            @pl.when(p == at)
            def _():
                forward_near(h)
        for at, h in FORWARD_FAR.items():
            @pl.when(p == at)
            def _():
                forward_far(h)

        nxt = jnp.minimum(p + 1, PAIRS - 1)

        @pl.when(p < PAIRS - 1)
        def _():
            before(nxt)

        score_step_next(p)
        value_step(p, 1, 1)

        for h in range(HPG):
            @pl.when(p == ORDER.index((h, 3, 1)))
            def _():
                send_part(h)

        for h in range(HPG - 1):
            @pl.when(p == ORDER.index((h, 3, 0)))
            def _():
                send_result(h)

        return carry

    def score_step_next(p):
        score_step(p + 1, 0, 0)

    lax.fori_loop(0, PAIRS - 1, pair, 0)
    p = PAIRS - 1
    score_step(p, 1, 1)
    value_step(p, 0, 0)
    value_step(p, 1, 1)
    send_result(HPG - 1)

    for h in range(HPG):
        await_bytes(o_out.at[h], o_recv.at[h])
    o_ref[...] = o_in[...]

    for kind in range(3):
        sent(kind, 2)
    for h in range(HPG):
        await_bytes(o_out.at[h, seven, :], o_send.at[h])
        await_bytes(part_out.at[h], part_sem.at[0, h, 0])
        await_bytes(lse_out.at[h], part_sem.at[0, h, 1])
        await_bytes(q_all.at[h, 0], q_send.at[h])
        for t, chunk in ((0, k_chunk), (1, v_chunk)):
            for i in range(3):
                await_bytes(chunk(h, 0, 0), kv_send.at[t, h, 0, i])
            for slot in (1, 2, 3):
                await_bytes(chunk(h, slot, 0), kv_send.at[t, h, slot, 0])
        await_bytes(k_chunk(h, 1, 0), kv_send.at[0, h, 1, 1])
        await_bytes(v_chunk(h, 2, 0), kv_send.at[1, h, 2, 1])


def shards(queries, keys, values, query_gain, key_gain):
    bf16, f32 = jnp.bfloat16, jnp.float32
    dma = pltpu.SemaphoreType.DMA
    width = queries.shape[1]
    halves = (HPG, 2, ROWS)
    return pl.pallas_call(
        kernel,
        out_shape=jax.ShapeDtypeStruct((TOK, width), bf16),
        in_specs=[pl.BlockSpec(memory_space=pltpu.VMEM)] * 5,
        out_specs=pl.BlockSpec(memory_space=pltpu.VMEM),
        scratch_shapes=[
            pltpu.VMEM((TOK, width), bf16),
            pltpu.VMEM((TOK, width), bf16),
            pltpu.VMEM((HPG, 4, KEYS, HEAD_DIM), bf16),
            pltpu.VMEM((HPG, 4, KEYS, 2 * HEAD_DIM), bf16),
            pltpu.VMEM((*halves, HEAD_DIM), bf16),
            pltpu.VMEM((2, BQ, KEYS), f32),
            pltpu.VMEM((2, BQ, 1), f32),
            pltpu.VMEM((2, BQ, 1), f32),
            pltpu.VMEM((*halves, 1), f32),
            pltpu.VMEM((*halves, 2 * HEAD_DIM), f32),
            pltpu.VMEM((HPG, ROWS, HEAD_DIM), bf16),
            pltpu.VMEM((HPG, ROWS, HEAD_DIM), bf16),
            pltpu.VMEM((HPG, 8, ROWS), f32),
            pltpu.VMEM((HPG, 8, ROWS), f32),
            pltpu.VMEM((HPG, ROWS, HEAD_DIM), bf16),
            pltpu.VMEM((TOK, width), bf16),
            dma((2, HPG, 4, 2)),
            dma((2, HPG, 4, 3)),
            dma((HPG, 2)),
            dma((HPG,)),
            dma((3, HPG)),
            dma((2, HPG, 2)),
            dma((HPG,)),
            dma((HPG,)),
        ],
        compiler_params=pltpu.CompilerParams(
            collective_id=0, has_side_effects=True, vmem_limit_bytes=60 << 20
        ),
    )(queries, keys, values, query_gain.reshape(1, width), key_gain.reshape(1, width))


def solution(mesh):
    rows = P(("blk", "head"), None)
    return jax.shard_map(
        shards, mesh=mesh, in_specs=(rows, rows, rows, P(), P()), out_specs=rows,
        check_vma=False,
    )
```

```python
import functools
import math

import jax
import jax.numpy as jnp
from jax import lax
from jax.experimental import pallas as pl
from jax.experimental.pallas import tpu as pltpu
from jax.sharding import PartitionSpec as P

HEAD_DIM = 128
EPS = 1e-06
HPG = 3
GROUPS = 8
TOK = 128
ROWS = TOK * GROUPS
BQ = 512
KEYS = 2 * ROWS
SCALE = math.log2(math.e) / math.sqrt(HEAD_DIM)
MESH = pl.DeviceIdType.MESH
PIECE = ROWS // 2
ORDER = (
    (0, 0, 0), (0, 1, 0), (0, 0, 1), (0, 2, 0), (0, 1, 1), (1, 0, 0),
    (0, 2, 1), (1, 0, 1), (1, 1, 0), (0, 3, 1), (1, 1, 1), (1, 2, 0),
    (1, 2, 1), (2, 0, 0), (2, 0, 1), (1, 3, 1), (2, 1, 0), (2, 1, 1),
    (0, 3, 0), (2, 2, 1), (2, 3, 1), (1, 3, 0), (2, 2, 0), (2, 3, 0),
)
PAIRS = len(ORDER)
FORWARD_NEAR = {0: (0, 0), 2: (0, 1), 6: (1, 0), 9: (1, 1), 13: (2, 0), 15: (2, 1)}
FORWARD_FAR = {7: 0, 13: 1, 17: 2}


def first_uses(key):
    seen, firsts = set(), []
    for p, entry in enumerate(ORDER):
        if key(entry) is not None and key(entry) not in seen:
            seen.add(key(entry))
            firsts.append(p)
    return firsts


CHUNK_FIRST = first_uses(lambda e: e[:2])
ACROSS_FIRST = first_uses(lambda e: e[0] if e[2] else None)


def one_of(u, options):
    return functools.reduce(jnp.logical_or, [u == o for o in options])


def place(p):
    def column(i):
        value = 0
        for v in sorted({e[i] for e in ORDER} - {0}):
            value = jnp.where(one_of(p, [n for n, e in enumerate(ORDER) if e[i] == v]), v, value)
        return value

    return column(1), column(0), column(2)


def normed(wide, gain):
    mean_sq = jnp.mean(wide * wide, axis=-1, keepdims=True)
    return (wide * lax.rsqrt(mean_sq + EPS) * gain).astype(jnp.bfloat16)


def kernel(
    q_in, k_in, v_in, qg_ref, kg_ref, o_ref,
    qn, kn, k_all, v_all, q_all, scores, shrink, peak, top, acc,
    part_out, part_in, lse_out, lse_in, o_out, o_in,
    kv_recv, kv_send, q_recv, q_send, in_send, part_sem, o_send, o_recv,
):
    b = lax.axis_index("blk")
    c = lax.axis_index("head")
    side = b // 8
    y = (b // 2) % 4
    core = b % 2
    other_core = (b + 1 - 2 * core, c)
    above = (side * 8 + ((y + 1) % 4) * 2 + core, c)
    below = (side * 8 + ((y + 3) % 4) * 2 + core, c)
    across = ((b + 8) % 16, c)

    def remote(src, dst, send, recv, dev):
        return pltpu.make_async_remote_copy(
            src_ref=src, dst_ref=dst, send_sem=send, recv_sem=recv,
            device_id=dev, device_id_type=MESH,
        )

    def await_bytes(ref, sem):
        pltpu.make_async_copy(ref, ref, sem).wait()

    def cols(n):
        return pl.ds(pl.multiple_of(n * HEAD_DIM, HEAD_DIM), HEAD_DIM)

    def rows_of(g):
        return pl.ds(pl.multiple_of(g * TOK, TOK), TOK)

    def k_chunk(h, slot, core_slot):
        return k_all.at[h, slot, pl.ds(core_slot * ROWS, ROWS), :]

    def v_chunk(h, slot, core_slot):
        return v_all.at[h, slot, pl.ds(core_slot * ROWS, ROWS), pl.ds(0, HEAD_DIM)]

    v_all[:, :, :, HEAD_DIM:] = jnp.ones((HPG, 4, KEYS, HEAD_DIM), jnp.bfloat16)

    barrier = pltpu.get_barrier_semaphore()
    partners = [(b, (c + d) % GROUPS) for d in range(1, GROUPS)]
    partners += [other_core, above, below, across]
    for dev in partners:
        pl.semaphore_signal(barrier, inc=1, device_id=dev, device_id_type=MESH)
    kn[...] = normed(k_in[...].astype(jnp.float32), kg_ref[...])
    qn[...] = normed(q_in[...].astype(jnp.float32), qg_ref[...])
    pl.semaphore_wait(barrier, len(partners))

    def scatter(src, dst_of, kind, recv, h):
        mine = pltpu.make_async_copy(
            src.at[:, cols(c * HPG + h)], dst_of(rows_of(c)), recv
        )
        mine.start()
        for d in range(1, GROUPS):
            g = (c + d) % GROUPS
            remote(
                src.at[:, cols(g * HPG + h)], dst_of(rows_of(c)),
                in_send.at[kind, h], recv, (b, g),
            ).start()

    def scatter_k(h):
        scatter(kn, lambda r: k_all.at[h, 0, r, :], 0, kv_recv.at[0, h, 0, 0], h)

    def scatter_v(h):
        scatter(
            v_in, lambda r: v_all.at[h, 0, r, pl.ds(0, HEAD_DIM)], 1,
            kv_recv.at[1, h, 0, 0], h,
        )

    def scatter_q(h):
        scatter(qn, lambda r: q_all.at[h, 0, r, :], 2, q_recv.at[h, 0], h)

    scatter_k(0)
    scatter_v(0)
    scatter_q(0)
    acc[...] = jnp.zeros_like(acc)
    top[...] = jnp.full_like(top, -1e30)

    def piece(t, h, slot, n):
        rows = pl.ds(n * PIECE, PIECE)
        if t == 0:
            return k_all.at[h, slot, rows, :]
        return v_all.at[h, slot, rows, pl.ds(0, HEAD_DIM)]

    def send_own(h):
        def near(t, n):
            mine = piece(t, h, 0, n)
            remote(mine, piece(t, h, 1 + n, 0), kv_send.at[t, h, 0, 1],
                   kv_recv.at[t, h, 1 + n, 0], above).start()
            remote(mine, piece(t, h, 1 + n, 1), kv_send.at[t, h, 0, 2],
                   kv_recv.at[t, h, 1 + n, 0], below).start()

        for t, chunk in ((0, k_chunk), (1, v_chunk)):
            mine = chunk(h, 0, 0)
            await_bytes(mine, kv_recv.at[t, h, 0, 0])
            near(t, 0)
            remote(mine, chunk(h, 0, 1), kv_send.at[t, h, 0, 0],
                   kv_recv.at[t, h, 0, 1], other_core).start()
        near(0, 1)
        near(1, 1)

    def send_across(h):
        await_bytes(q_all.at[h, 0], q_recv.at[h, 0])
        remote(q_all.at[h, 0], q_all.at[h, 1], q_send.at[h],
               q_recv.at[h, 1], across).start()

    def to_other_core(t, h, slot):
        chunk = (k_chunk, v_chunk)[t]
        remote(chunk(h, slot, 0), chunk(h, slot, 1), kv_send.at[t, h, slot, 0],
               kv_recv.at[t, h, slot, 1], other_core).start()

    def forward_near(h, n):
        for t, chunk in ((0, k_chunk), (1, v_chunk)):
            await_bytes(chunk(h, 1 + n, 0), kv_recv.at[t, h, 1 + n, 0])
            to_other_core(t, h, 1 + n)
        remote(piece(0, h, 1 + n, 0), piece(0, h, 3, n), kv_send.at[0, h, 1, 1],
               kv_recv.at[0, h, 3, 0], above).start()
        remote(piece(1, h, 1 + n, 1), piece(1, h, 3, n), kv_send.at[1, h, 2, 1],
               kv_recv.at[1, h, 3, 0], below).start()

    def forward_far(h):
        for t, chunk in ((0, k_chunk), (1, v_chunk)):
            await_bytes(chunk(h, 3, 0), kv_recv.at[t, h, 3, 0])
            to_other_core(t, h, 3)

    def score_step(p, block, slot):
        chunk, h, half = place(p)
        rows = pl.ds(block * BQ, BQ)
        s = lax.dot_general(
            q_all[h, half, rows, :], k_all[h, chunk], (((1,), (1,)), ((), ())),
            preferred_element_type=jnp.float32,
        )
        scores[slot] = s
        old = top[h, half, rows, :]
        new = jnp.maximum(old, jnp.max(s, axis=1, keepdims=True))
        top[h, half, rows, :] = new
        peak[slot] = new * SCALE
        shrink[slot] = jnp.exp2((old - new) * SCALE)

    def value_step(p, block, slot):
        chunk, h, half = place(p)
        rows = pl.ds(block * BQ, BQ)
        weights = jnp.exp2(scores[slot] * SCALE - peak[slot])
        mixed = jnp.dot(
            weights.astype(jnp.bfloat16), v_all[h, chunk],
            preferred_element_type=jnp.float32,
        )
        acc[h, half, rows, :] = acc[h, half, rows, :] * shrink[slot] + mixed

    def before(p):
        chunk, h, half = place(p)

        @pl.when(one_of(p, CHUNK_FIRST))
        def _():
            await_bytes(k_chunk(h, chunk, 1), kv_recv.at[0, h, chunk, 1])
            await_bytes(v_chunk(h, chunk, 1), kv_recv.at[1, h, chunk, 1])

        @pl.when(one_of(p, ACROSS_FIRST))
        def _():
            await_bytes(q_all.at[h, 1], q_recv.at[h, 1])

    def finish_block(h, half, block):
        rows = pl.ds(block * BQ, BQ)
        total = acc[h, half, rows, HEAD_DIM:]
        mean = acc[h, half, rows, :HEAD_DIM] / total
        lse = top[h, half, rows, :] * SCALE + jnp.log2(total)
        return mean, lse

    def send_part(h):
        for block in range(ROWS // BQ):
            rows = pl.ds(block * BQ, BQ)
            mean, lse = finish_block(h, 1, block)
            part_out[h, rows, :] = mean.astype(jnp.bfloat16)
            lse_out[h, :, rows] = jnp.transpose(lse)[:8]
        remote(part_out.at[h], part_in.at[h], part_sem.at[0, h, 0],
               part_sem.at[1, h, 0], across).start()
        remote(lse_out.at[h], lse_in.at[h], part_sem.at[0, h, 1],
               part_sem.at[1, h, 1], across).start()

    def send_result(h, block):
        if block == 0:
            await_bytes(part_in.at[h], part_sem.at[1, h, 0])
            await_bytes(lse_in.at[h], part_sem.at[1, h, 1])
        rows = pl.ds(block * BQ, BQ)
        mean, lse = finish_block(h, 0, block)
        row = jnp.broadcast_to(lse_in[h, 0:1, rows], (HEAD_DIM, BQ))
        lse2 = jnp.transpose(row)
        high = jnp.maximum(lse, lse2)
        w1 = jnp.exp2(lse - high)
        w2 = jnp.exp2(lse2 - high)
        both = mean * w1 + part_in[h, rows, :].astype(jnp.float32) * w2
        o_out[h, rows, :] = (both / (w1 + w2)).astype(jnp.bfloat16)
        target = cols(c * HPG + h)
        for g in range(block * BQ // TOK, (block + 1) * BQ // TOK):
            @pl.when(g == c)
            def _():
                pltpu.make_async_copy(
                    o_out.at[h, rows_of(c), :], o_in.at[:, target], o_recv.at[h]
                ).start()

            @pl.when(g != c)
            def _():
                remote(o_out.at[h, rows_of(g), :], o_in.at[:, target],
                       o_send.at[h], o_recv.at[h], (b, g)).start()

    seven = pl.ds(0, (GROUPS - 1) * TOK)

    def sent(kind, h):
        await_bytes(o_out.at[h, seven, :], in_send.at[kind, h])

    send_own(0)
    sent(0, 0)
    sent(1, 0)
    scatter_k(1)
    send_across(0)
    sent(2, 0)
    scatter_v(1)
    scatter_q(1)
    scatter_k(2)
    scatter_v(2)
    scatter_q(2)
    before(0)
    score_step(0, 0, 0)

    def pair(p, carry):
        score_step(p, 1, 1)
        value_step(p, 0, 0)

        for at, (h, n) in FORWARD_NEAR.items():
            @pl.when(p == at)
            def _():
                forward_near(h, n)

        @pl.when(p == 3)
        def _():
            send_own(1)
            send_across(1)

        @pl.when(p == 8)
        def _():
            send_own(2)
            send_across(2)

        for at, h in FORWARD_FAR.items():
            @pl.when(p == at)
            def _():
                forward_far(h)

        nxt = jnp.minimum(p + 1, PAIRS - 1)

        @pl.when(p < PAIRS - 1)
        def _():
            before(nxt)

        score_step_next(p)
        value_step(p, 1, 1)

        for h in range(HPG):
            @pl.when(p == ORDER.index((h, 3, 1)))
            def _():
                send_part(h)

        for h in range(HPG - 1):
            @pl.when(p == ORDER.index((h, 3, 0)))
            def _():
                send_result(h, 0)
                send_result(h, 1)

        return carry

    def score_step_next(p):
        score_step(p + 1, 0, 0)

    lax.fori_loop(0, PAIRS - 1, pair, 0)
    p = PAIRS - 1
    score_step(p, 1, 1)
    value_step(p, 0, 0)
    send_result(HPG - 1, 0)
    value_step(p, 1, 1)
    send_result(HPG - 1, 1)

    for h in range(HPG):
        await_bytes(o_out.at[h], o_recv.at[h])
    o_ref[...] = o_in[...]

    for kind in range(3):
        sent(kind, 1)
        sent(kind, 2)
    for h in range(HPG):
        await_bytes(o_out.at[h, seven, :], o_send.at[h])
        await_bytes(part_out.at[h], part_sem.at[0, h, 0])
        await_bytes(lse_out.at[h], part_sem.at[0, h, 1])
        await_bytes(q_all.at[h, 0], q_send.at[h])
        for t, chunk in ((0, k_chunk), (1, v_chunk)):
            for i in range(3):
                await_bytes(chunk(h, 0, 0), kv_send.at[t, h, 0, i])
            for slot in (1, 2, 3):
                await_bytes(chunk(h, slot, 0), kv_send.at[t, h, slot, 0])
        await_bytes(k_chunk(h, 1, 0), kv_send.at[0, h, 1, 1])
        await_bytes(v_chunk(h, 2, 0), kv_send.at[1, h, 2, 1])


def shards(queries, keys, values, query_gain, key_gain):
    bf16, f32 = jnp.bfloat16, jnp.float32
    dma = pltpu.SemaphoreType.DMA
    width = queries.shape[1]
    halves = (HPG, 2, ROWS)
    return pl.pallas_call(
        kernel,
        out_shape=jax.ShapeDtypeStruct((TOK, width), bf16),
        in_specs=[pl.BlockSpec(memory_space=pltpu.VMEM)] * 5,
        out_specs=pl.BlockSpec(memory_space=pltpu.VMEM),
        scratch_shapes=[
            pltpu.VMEM((TOK, width), bf16),
            pltpu.VMEM((TOK, width), bf16),
            pltpu.VMEM((HPG, 4, KEYS, HEAD_DIM), bf16),
            pltpu.VMEM((HPG, 4, KEYS, 2 * HEAD_DIM), bf16),
            pltpu.VMEM((*halves, HEAD_DIM), bf16),
            pltpu.VMEM((2, BQ, KEYS), f32),
            pltpu.VMEM((2, BQ, 1), f32),
            pltpu.VMEM((2, BQ, 1), f32),
            pltpu.VMEM((*halves, 1), f32),
            pltpu.VMEM((*halves, 2 * HEAD_DIM), f32),
            pltpu.VMEM((HPG, ROWS, HEAD_DIM), bf16),
            pltpu.VMEM((HPG, ROWS, HEAD_DIM), bf16),
            pltpu.VMEM((HPG, 8, ROWS), f32),
            pltpu.VMEM((HPG, 8, ROWS), f32),
            pltpu.VMEM((HPG, ROWS, HEAD_DIM), bf16),
            pltpu.VMEM((TOK, width), bf16),
            dma((2, HPG, 4, 2)),
            dma((2, HPG, 4, 3)),
            dma((HPG, 2)),
            dma((HPG,)),
            dma((3, HPG)),
            dma((2, HPG, 2)),
            dma((HPG,)),
            dma((HPG,)),
        ],
        compiler_params=pltpu.CompilerParams(
            collective_id=0, has_side_effects=True, vmem_limit_bytes=60 << 20
        ),
    )(queries, keys, values, query_gain.reshape(1, width), key_gain.reshape(1, width))


def solution(mesh):
    rows = P(("blk", "head"), None)
    return jax.shard_map(
        shards, mesh=mesh, in_specs=(rows, rows, rows, P(), P()), out_specs=rows,
        check_vma=False,
    )
```

```python
import functools
import math

import jax
import jax.numpy as jnp
from jax import lax
from jax.experimental import pallas as pl
from jax.experimental.pallas import tpu as pltpu
from jax.sharding import PartitionSpec as P

HEAD_DIM = 128
EPS = 1e-06
HPG = 3
GROUPS = 8
TOK = 128
ROWS = TOK * GROUPS
BQ = 512
KEYS = 2 * ROWS
SCALE = math.log2(math.e) / math.sqrt(HEAD_DIM)
MESH = pl.DeviceIdType.MESH
PIECE = ROWS // 2
ORDER = (
    (0, 0, 0), (0, 1, 0), (0, 0, 1), (0, 2, 0), (0, 1, 1), (1, 0, 0),
    (0, 2, 1), (1, 0, 1), (1, 1, 0), (0, 3, 1), (1, 1, 1), (1, 2, 0),
    (1, 2, 1), (2, 0, 0), (2, 0, 1), (1, 3, 1), (2, 1, 0), (2, 1, 1),
    (0, 3, 0), (2, 2, 1), (2, 3, 1), (1, 3, 0), (2, 2, 0), (2, 3, 0),
)
PAIRS = len(ORDER)
FORWARD_NEAR = {0: (0, 0), 2: (0, 1), 6: (1, 0), 9: (1, 1), 13: (2, 0), 15: (2, 1)}
FORWARD_FAR = {7: 0, 13: 1, 17: 2}


def first_uses(key):
    seen, firsts = set(), []
    for p, entry in enumerate(ORDER):
        if key(entry) is not None and key(entry) not in seen:
            seen.add(key(entry))
            firsts.append(p)
    return firsts


CHUNK_FIRST = first_uses(lambda e: e[:2])
ACROSS_FIRST = first_uses(lambda e: e[0] if e[2] else None)


def one_of(u, options):
    return functools.reduce(jnp.logical_or, [u == o for o in options])


def place(p):
    def column(i):
        value = 0
        for v in sorted({e[i] for e in ORDER} - {0}):
            value = jnp.where(one_of(p, [n for n, e in enumerate(ORDER) if e[i] == v]), v, value)
        return value

    return column(1), column(0), column(2)


def normed(wide, gain):
    mean_sq = jnp.mean(wide * wide, axis=-1, keepdims=True)
    return (wide * lax.rsqrt(mean_sq + EPS) * gain).astype(jnp.bfloat16)


def kernel(
    q_in, k_in, v_in, qg_ref, kg_ref, o_ref,
    qn, kn, k_all, v_all, q_all, scores, shrink, peak, top, acc,
    part_out, part_in, lse_out, lse_in, o_out, o_in,
    kv_recv, kv_send, q_recv, q_send, in_send, part_sem, o_send, o_recv,
):
    b = lax.axis_index("blk")
    c = lax.axis_index("head")
    side = b // 8
    y = (b // 2) % 4
    core = b % 2
    other_core = (b + 1 - 2 * core, c)
    above = (side * 8 + ((y + 1) % 4) * 2 + core, c)
    below = (side * 8 + ((y + 3) % 4) * 2 + core, c)
    across = ((b + 8) % 16, c)

    def remote(src, dst, send, recv, dev):
        return pltpu.make_async_remote_copy(
            src_ref=src, dst_ref=dst, send_sem=send, recv_sem=recv,
            device_id=dev, device_id_type=MESH,
        )

    def await_bytes(ref, sem):
        pltpu.make_async_copy(ref, ref, sem).wait()

    def cols(n):
        return pl.ds(pl.multiple_of(n * HEAD_DIM, HEAD_DIM), HEAD_DIM)

    def rows_of(g):
        return pl.ds(pl.multiple_of(g * TOK, TOK), TOK)

    def k_chunk(h, slot, core_slot):
        return k_all.at[h, slot, pl.ds(core_slot * ROWS, ROWS), :]

    def v_chunk(h, slot, core_slot):
        return v_all.at[h, slot, pl.ds(core_slot * ROWS, ROWS), pl.ds(0, HEAD_DIM)]

    v_all[:, :, :, HEAD_DIM:] = jnp.ones((HPG, 4, KEYS, HEAD_DIM), jnp.bfloat16)

    barrier = pltpu.get_barrier_semaphore()
    partners = [(b, (c + d) % GROUPS) for d in range(1, GROUPS)]
    partners += [other_core, above, below, across]
    for dev in partners:
        pl.semaphore_signal(barrier, inc=1, device_id=dev, device_id_type=MESH)
    kn[...] = normed(k_in[...].astype(jnp.float32), kg_ref[...])
    qn[...] = normed(q_in[...].astype(jnp.float32), qg_ref[...])
    pl.semaphore_wait(barrier, len(partners))

    def scatter(src, dst_of, kind, recv, h):
        mine = pltpu.make_async_copy(
            src.at[:, cols(c * HPG + h)], dst_of(rows_of(c)), recv
        )
        mine.start()
        for d in range(1, GROUPS):
            g = (c + d) % GROUPS
            remote(
                src.at[:, cols(g * HPG + h)], dst_of(rows_of(c)),
                in_send.at[kind, h], recv, (b, g),
            ).start()

    def scatter_k(h):
        scatter(kn, lambda r: k_all.at[h, 0, r, :], 0, kv_recv.at[0, h, 0, 0], h)

    def scatter_v(h):
        scatter(
            v_in, lambda r: v_all.at[h, 0, r, pl.ds(0, HEAD_DIM)], 1,
            kv_recv.at[1, h, 0, 0], h,
        )

    def scatter_q(h):
        scatter(qn, lambda r: q_all.at[h, 0, r, :], 2, q_recv.at[h, 0], h)

    scatter_k(0)
    scatter_v(0)
    scatter_q(0)
    acc[...] = jnp.zeros_like(acc)
    top[...] = jnp.full_like(top, -1e30)

    def piece(t, h, slot, n):
        rows = pl.ds(n * PIECE, PIECE)
        if t == 0:
            return k_all.at[h, slot, rows, :]
        return v_all.at[h, slot, rows, pl.ds(0, HEAD_DIM)]

    def send_own(h):
        def near(t, n):
            mine = piece(t, h, 0, n)
            remote(mine, piece(t, h, 1 + n, 0), kv_send.at[t, h, 0, 1],
                   kv_recv.at[t, h, 1 + n, 0], above).start()
            remote(mine, piece(t, h, 1 + n, 1), kv_send.at[t, h, 0, 2],
                   kv_recv.at[t, h, 1 + n, 0], below).start()

        for t, chunk in ((0, k_chunk), (1, v_chunk)):
            mine = chunk(h, 0, 0)
            await_bytes(mine, kv_recv.at[t, h, 0, 0])
            near(t, 0)
            remote(mine, chunk(h, 0, 1), kv_send.at[t, h, 0, 0],
                   kv_recv.at[t, h, 0, 1], other_core).start()
        near(0, 1)
        near(1, 1)

    def send_across(h):
        await_bytes(q_all.at[h, 0], q_recv.at[h, 0])
        remote(q_all.at[h, 0], q_all.at[h, 1], q_send.at[h],
               q_recv.at[h, 1], across).start()

    def to_other_core(t, h, slot):
        chunk = (k_chunk, v_chunk)[t]
        remote(chunk(h, slot, 0), chunk(h, slot, 1), kv_send.at[t, h, slot, 0],
               kv_recv.at[t, h, slot, 1], other_core).start()

    def forward_near(h, n):
        for t, chunk in ((0, k_chunk), (1, v_chunk)):
            await_bytes(chunk(h, 1 + n, 0), kv_recv.at[t, h, 1 + n, 0])
            to_other_core(t, h, 1 + n)
        remote(piece(0, h, 1 + n, 0), piece(0, h, 3, n), kv_send.at[0, h, 1, 1],
               kv_recv.at[0, h, 3, 0], above).start()
        remote(piece(1, h, 1 + n, 1), piece(1, h, 3, n), kv_send.at[1, h, 2, 1],
               kv_recv.at[1, h, 3, 0], below).start()

    def forward_far(h):
        for t, chunk in ((0, k_chunk), (1, v_chunk)):
            await_bytes(chunk(h, 3, 0), kv_recv.at[t, h, 3, 0])
            to_other_core(t, h, 3)

    def score_step(p, block, slot):
        chunk, h, half = place(p)
        rows = pl.ds(block * BQ, BQ)
        s = lax.dot_general(
            q_all[h, half, rows, :], k_all[h, chunk], (((1,), (1,)), ((), ())),
            preferred_element_type=jnp.float32,
        )
        scores[slot] = s
        old = top[h, half, rows, :]
        new = jnp.maximum(old, jnp.max(s, axis=1, keepdims=True))
        top[h, half, rows, :] = new
        peak[slot] = new * SCALE
        shrink[slot] = jnp.exp2((old - new) * SCALE)

    def value_step(p, block, slot):
        chunk, h, half = place(p)
        rows = pl.ds(block * BQ, BQ)
        weights = jnp.exp2(scores[slot] * SCALE - peak[slot])
        mixed = jnp.dot(
            weights.astype(jnp.bfloat16), v_all[h, chunk],
            preferred_element_type=jnp.float32,
        )
        acc[h, half, rows, :] = acc[h, half, rows, :] * shrink[slot] + mixed

    def before(p):
        chunk, h, half = place(p)

        @pl.when(one_of(p, CHUNK_FIRST))
        def _():
            await_bytes(k_chunk(h, chunk, 1), kv_recv.at[0, h, chunk, 1])
            await_bytes(v_chunk(h, chunk, 1), kv_recv.at[1, h, chunk, 1])

        @pl.when(one_of(p, ACROSS_FIRST))
        def _():
            await_bytes(q_all.at[h, 1], q_recv.at[h, 1])

    def finish_block(h, half, block):
        rows = pl.ds(block * BQ, BQ)
        total = acc[h, half, rows, HEAD_DIM:]
        mean = acc[h, half, rows, :HEAD_DIM] / total
        lse = top[h, half, rows, :] * SCALE + jnp.log2(total)
        return mean, lse

    def send_part(h):
        for block in range(ROWS // BQ):
            rows = pl.ds(block * BQ, BQ)
            mean, lse = finish_block(h, 1, block)
            part_out[h, rows, :] = mean.astype(jnp.bfloat16)
            lse_out[h, :, rows] = jnp.transpose(lse)[:8]
        remote(part_out.at[h], part_in.at[h], part_sem.at[0, h, 0],
               part_sem.at[1, h, 0], across).start()
        remote(lse_out.at[h], lse_in.at[h], part_sem.at[0, h, 1],
               part_sem.at[1, h, 1], across).start()

    def send_result(h, block):
        if block == 0:
            await_bytes(part_in.at[h], part_sem.at[1, h, 0])
            await_bytes(lse_in.at[h], part_sem.at[1, h, 1])
        rows = pl.ds(block * BQ, BQ)
        mean, lse = finish_block(h, 0, block)
        row = jnp.broadcast_to(lse_in[h, 0:1, rows], (HEAD_DIM, BQ))
        lse2 = jnp.transpose(row)
        high = jnp.maximum(lse, lse2)
        w1 = jnp.exp2(lse - high)
        w2 = jnp.exp2(lse2 - high)
        both = mean * w1 + part_in[h, rows, :].astype(jnp.float32) * w2
        o_out[h, rows, :] = (both / (w1 + w2)).astype(jnp.bfloat16)
        target = cols(c * HPG + h)
        for g in range(block * BQ // TOK, (block + 1) * BQ // TOK):
            @pl.when(g == c)
            def _():
                pltpu.make_async_copy(
                    o_out.at[h, rows_of(c), :], o_in.at[:, target], o_recv.at[h]
                ).start()

            @pl.when(g != c)
            def _():
                remote(o_out.at[h, rows_of(g), :], o_in.at[:, target],
                       o_send.at[h], o_recv.at[h], (b, g)).start()

    seven = pl.ds(0, (GROUPS - 1) * TOK)

    def sent(kind, h):
        await_bytes(o_out.at[h, seven, :], in_send.at[kind, h])

    send_own(0)
    sent(0, 0)
    sent(1, 0)
    scatter_k(1)
    send_across(0)
    sent(2, 0)
    scatter_v(1)
    scatter_q(1)
    before(0)
    score_step(0, 0, 0)

    def pair(p, carry):
        score_step(p, 1, 1)
        value_step(p, 0, 0)

        @pl.when(p == 0)
        def _():
            scatter_k(2)
            scatter_v(2)
            scatter_q(2)

        for at, (h, n) in FORWARD_NEAR.items():
            @pl.when(p == at)
            def _():
                forward_near(h, n)

        @pl.when(p == 3)
        def _():
            send_own(1)
            send_across(1)

        @pl.when(p == 8)
        def _():
            send_own(2)
            send_across(2)

        for at, h in FORWARD_FAR.items():
            @pl.when(p == at)
            def _():
                forward_far(h)

        nxt = jnp.minimum(p + 1, PAIRS - 1)

        @pl.when(p < PAIRS - 1)
        def _():
            before(nxt)

        score_step_next(p)
        value_step(p, 1, 1)

        for h in range(HPG):
            @pl.when(p == ORDER.index((h, 3, 1)))
            def _():
                send_part(h)

        for h in range(HPG - 1):
            @pl.when(p == ORDER.index((h, 3, 0)))
            def _():
                send_result(h, 0)
                send_result(h, 1)

        return carry

    def score_step_next(p):
        score_step(p + 1, 0, 0)

    lax.fori_loop(0, PAIRS - 1, pair, 0)
    p = PAIRS - 1
    score_step(p, 1, 1)
    value_step(p, 0, 0)
    send_result(HPG - 1, 0)
    value_step(p, 1, 1)
    send_result(HPG - 1, 1)

    for h in range(HPG):
        await_bytes(o_out.at[h], o_recv.at[h])
    o_ref[...] = o_in[...]

    for kind in range(3):
        sent(kind, 1)
        sent(kind, 2)
    for h in range(HPG):
        await_bytes(o_out.at[h, seven, :], o_send.at[h])
        await_bytes(part_out.at[h], part_sem.at[0, h, 0])
        await_bytes(lse_out.at[h], part_sem.at[0, h, 1])
        await_bytes(q_all.at[h, 0], q_send.at[h])
        for t, chunk in ((0, k_chunk), (1, v_chunk)):
            for i in range(3):
                await_bytes(chunk(h, 0, 0), kv_send.at[t, h, 0, i])
            for slot in (1, 2, 3):
                await_bytes(chunk(h, slot, 0), kv_send.at[t, h, slot, 0])
        await_bytes(k_chunk(h, 1, 0), kv_send.at[0, h, 1, 1])
        await_bytes(v_chunk(h, 2, 0), kv_send.at[1, h, 2, 1])


def shards(queries, keys, values, query_gain, key_gain):
    bf16, f32 = jnp.bfloat16, jnp.float32
    dma = pltpu.SemaphoreType.DMA
    width = queries.shape[1]
    halves = (HPG, 2, ROWS)
    return pl.pallas_call(
        kernel,
        out_shape=jax.ShapeDtypeStruct((TOK, width), bf16),
        in_specs=[pl.BlockSpec(memory_space=pltpu.VMEM)] * 5,
        out_specs=pl.BlockSpec(memory_space=pltpu.VMEM),
        scratch_shapes=[
            pltpu.VMEM((TOK, width), bf16),
            pltpu.VMEM((TOK, width), bf16),
            pltpu.VMEM((HPG, 4, KEYS, HEAD_DIM), bf16),
            pltpu.VMEM((HPG, 4, KEYS, 2 * HEAD_DIM), bf16),
            pltpu.VMEM((*halves, HEAD_DIM), bf16),
            pltpu.VMEM((2, BQ, KEYS), f32),
            pltpu.VMEM((2, BQ, 1), f32),
            pltpu.VMEM((2, BQ, 1), f32),
            pltpu.VMEM((*halves, 1), f32),
            pltpu.VMEM((*halves, 2 * HEAD_DIM), f32),
            pltpu.VMEM((HPG, ROWS, HEAD_DIM), bf16),
            pltpu.VMEM((HPG, ROWS, HEAD_DIM), bf16),
            pltpu.VMEM((HPG, 8, ROWS), f32),
            pltpu.VMEM((HPG, 8, ROWS), f32),
            pltpu.VMEM((HPG, ROWS, HEAD_DIM), bf16),
            pltpu.VMEM((TOK, width), bf16),
            dma((2, HPG, 4, 2)),
            dma((2, HPG, 4, 3)),
            dma((HPG, 2)),
            dma((HPG,)),
            dma((3, HPG)),
            dma((2, HPG, 2)),
            dma((HPG,)),
            dma((HPG,)),
        ],
        compiler_params=pltpu.CompilerParams(
            collective_id=0, has_side_effects=True, vmem_limit_bytes=60 << 20
        ),
    )(queries, keys, values, query_gain.reshape(1, width), key_gain.reshape(1, width))


def solution(mesh):
    rows = P(("blk", "head"), None)
    return jax.shard_map(
        shards, mesh=mesh, in_specs=(rows, rows, rows, P(), P()), out_specs=rows,
        check_vma=False,
    )
```
